32 devices in a mesh: row: 4 (over y, x), col: 8 (over z, core).
Axes of the slice: x: 2, y: 2, z: 4, core: 2. Of those that a mesh axis runs over, the one named last changes fastest.
Arguments:
- event_bins: bfloat16 [2048, 64], P(('row', 'col')), may hold values from -15 to 15
- counts: int32 [2048], P(('row', 'col')), may hold values from 1 to 8
- hidden_weight: bfloat16 [64, 1024], replicated, may hold values from -0.75 to 0.75
- hidden_bias: float32 [1024], replicated, may hold values from -4 to 4
- feature_weight: bfloat16 [1024, 256], replicated, may hold values from -0.1875 to 0.1875
Outputs:
- factor: float32 [2048, 2048], P('row', 'col')
The draws below stay inside these ranges and needn't reach their ends.
All inputs are finite; a program needn't handle non-finite values.
Results may differ from the reference program's by a relative error of at most 0.0037.
Values may be sent and summed in bfloat16 or wider, within the bound.
A program may use at most 64 MiB of HBM per device.

```python
import math
import jax
import jax.numpy as jnp
from jax import lax

D_IN = 64
HID = 1024
FEAT = 256
TILE = 512
NW = 2048
PW = 256
N_ROW = 4


def draw_event_bins(key, part):
    key_scale = jax.random.fold_in(key, 11)
    key_entries = jax.random.fold_in(key, 12)
    scales = jnp.exp(jax.random.uniform(key_scale, (NW, 1), jnp.float32, math.log(0.25), math.log(2.5)))
    entries = jax.random.normal(key_entries, (NW, D_IN), jnp.float32)
    return jnp.clip(entries * scales, -15.0, 15.0).astype(jnp.bfloat16)


def plant(drawn, own_key, least, largest):
    longest = drawn.shape.index(max(drawn.shape))
    spots = []
    for shift in (0, 1):
        where = [jax.random.randint(jax.random.fold_in(own_key, axis), (), 0, length) for axis, length in enumerate(drawn.shape)]
        where[longest] = (where[longest] + shift) % drawn.shape[longest]
        spots.append(tuple(where))
    return drawn.at[spots[0]].set(least).at[spots[1]].set(largest)


def gaussian(own_key, extent, width, reach, kind=jnp.bfloat16):
    return jnp.clip(width * jax.random.normal(own_key, extent, jnp.float32), -reach, reach).astype(kind)


def setup_inputs(seed: int = 0) -> dict:
    streams_of = jax.random.split(jax.random.key(seed), 6)
    return {
        "event_bins": draw_event_bins(jax.random.fold_in(streams_of[5], 71), 0),
        "counts": plant(jax.random.randint(streams_of[1], (NW,), 1, 9), jax.random.fold_in(streams_of[1], 1), 1, 8).astype(jnp.int32),
        "hidden_weight": gaussian(streams_of[2], (D_IN, HID), D_IN ** -0.5, 0.75),
        "hidden_bias": gaussian(streams_of[3], (HID,), 1.0, 4.0, jnp.float32),
        "feature_weight": gaussian(streams_of[4], (HID, FEAT), HID ** -0.5, 0.1875),
    }


kernel_offset = 0.25
root_five = 5.0 ** 0.5
best_precision = lax.Precision.HIGHEST

def embed_rows(bin_rows, hidden_weight, hidden_bias, feature_weight):
    preact = jnp.dot(bin_rows.astype(jnp.float32), hidden_weight.astype(jnp.float32), preferred_element_type=jnp.float32) + hidden_bias
    hidden = jax.nn.gelu(preact).astype(jnp.bfloat16)
    return jnp.dot(hidden.astype(jnp.float32), feature_weight.astype(jnp.float32), preferred_element_type=jnp.float32)

def kernel_block(left_feats, left_scale, right_feats, right_scale, left_start, right_start):
    inner_prod = lax.dot_general(left_feats, right_feats, (((1,), (1,)), ((), ())), precision=best_precision)
    left_sq = lax.optimization_barrier(jnp.sum(left_feats * left_feats, axis=1))
    right_sq = lax.optimization_barrier(jnp.sum(right_feats * right_feats, axis=1))
    dist_sq = jnp.maximum(left_sq[:, None] + right_sq[None, :] - 2.0 * inner_prod, 0.0)
    radius_sq = dist_sq * (4.0 / left_feats.shape[1])
    radius = jnp.sqrt(radius_sq)
    matern = (1.0 + root_five * radius + 5.0 / 3.0 * radius_sq) * jnp.exp(-root_five * radius)
    left_ids = left_start + jnp.arange(left_feats.shape[0], dtype=jnp.int32)
    right_ids = right_start + jnp.arange(right_feats.shape[0], dtype=jnp.int32)
    identity = (left_ids[:, None] == right_ids[None, :]).astype(jnp.float32)
    return identity + left_scale[:, None] * right_scale[None, :] * (matern + kernel_offset)

def reference(event_bins, counts, hidden_weight, hidden_bias, feature_weight):
    features = embed_rows(event_bins, hidden_weight, hidden_bias, feature_weight)
    scales = jnp.sqrt(counts.astype(jnp.float32))
    lead_width = 2 * PW
    leading = kernel_block(features, scales, features[:lead_width], scales[:lead_width], 0, 0)
    first_factor = jnp.linalg.cholesky(leading[:PW, :PW])
    first_panel = lax.linalg.triangular_solve(first_factor, leading[:, :PW], left_side=False, lower=True, transpose_a=True)
    second_cols = leading[:, PW:] - jnp.dot(first_panel, first_panel[PW:lead_width].T, precision=best_precision)
    second_factor = jnp.linalg.cholesky(second_cols[PW:lead_width])
    second_panel = lax.linalg.triangular_solve(second_factor, second_cols, left_side=False, lower=True, transpose_a=True)
    stacked = jnp.concatenate([first_panel, second_panel], axis=1)
    first_out = first_panel.at[:PW].set(jnp.tril(first_factor))
    second_out = jnp.concatenate([jnp.zeros((PW, PW), jnp.float32), jnp.tril(second_factor), second_panel[lead_width:]], axis=0)

    def one_block(block_index):
        start_row = block_index * TILE
        block_feats = lax.dynamic_slice_in_dim(features, start_row, TILE, 0)
        block_scales = lax.dynamic_slice_in_dim(scales, start_row, TILE, 0)
        block_stack = lax.dynamic_slice_in_dim(stacked, start_row, TILE, 0)
        full_rows = kernel_block(block_feats, block_scales, features, scales, start_row, 0)
        full_rows = full_rows - lax.dot_general(block_stack, stacked, (((1,), (1,)), ((), ())), precision=best_precision)
        row_ids = start_row + jnp.arange(TILE, dtype=jnp.int32)
        trailing = jnp.where(row_ids[:, None] >= lead_width, full_rows[:, lead_width:], 0.0)
        return jnp.concatenate([lax.dynamic_slice_in_dim(first_out, start_row, TILE, 0), lax.dynamic_slice_in_dim(second_out, start_row, TILE, 0), trailing], axis=1)
    blocks = lax.map(one_block, jnp.arange(N_ROW, dtype=jnp.int32))
    return blocks.reshape(NW, NW)
```

```python
import jax
import jax.numpy as jnp
from jax import lax
from jax.experimental import pallas as pl
from jax.experimental.pallas import tpu as pltpu
from jax.sharding import PartitionSpec as P

kernel_offset = 0.25
root_five = 5.0**0.5
BLK = 128
SUP = 32
SUB = 8
F32 = jnp.float32
BF16 = jnp.bfloat16


def split(x):
    hi = x.astype(BF16)
    return hi, (x - hi.astype(F32)).astype(BF16)


def dot_nt(a, b):
    return lax.dot_general(a, b, (((1,), (1,)), ((), ())), preferred_element_type=F32)


def dot3(a, b):
    return dot_nt(a[0], b[0]) + (dot_nt(a[0], b[1]) + dot_nt(a[1], b[0]))


def spread(x, j):
    return jnp.broadcast_to(x[j : j + 1, :], x.shape)

def eliminate(left, right, base):
    groups = len(left)
    left, right = list(left), list(right)
    sub = lax.broadcasted_iota(jnp.int32, (SUB, BLK), 0)
    out = []
    for k in range(groups):
        col = {}
        for t in range(k, groups):
            for m in range(SUB):
                lane = base + k * SUB + m
                col[t, m] = jnp.broadcast_to(left[t][:, lane : lane + 1], (SUB, BLK))
        keep = [None, None]
        for j in range(0, SUB, 2):
            a, b = col[k, j], col[k, j + 1]
            p, q, r = spread(a, j), spread(a, j + 1), spread(b, j + 1)
            det = p * r - q * q
            ip, ih = lax.rsqrt(p), lax.rsqrt(det)
            ip_ih = ip * ih
            alpha, beta = r * a - q * b, p * b - q * a
            ih2 = ih * ih
            la, lb = {k: a * ip}, {k: beta * ip_ih}
            for t in range(k + 1, groups):
                la[t] = col[t, j] * ip
                lb[t] = (p * col[t, j + 1] - q * col[t, j]) * ip_ih
            for m in range(j + 2, SUB):
                both = alpha * spread(a, m) + beta * spread(b, m)
                col[k, m] = col[k, m] - both * ih2
                if k + 1 < groups:
                    sa, sb = spread(la[k], m), spread(lb[k], m)
                    for t in range(k + 1, groups):
                        col[t, m] = col[t, m] - (la[t] * sa + lb[t] * sb)
            for h, side in enumerate((left, right)):
                first, second = spread(side[k], j), spread(side[k], j + 1)
                ua = first * ip
                ub = (p * second - q * first) * ip_ih
                keep[h] = ua if j == 0 else jnp.where(sub == j, ua, keep[h])
                keep[h] = jnp.where(sub == j + 1, ub, keep[h])
                for t in range(k if j + 2 < SUB else k + 1, groups):
                    side[t] = side[t] - (la[t] * ua + lb[t] * ub)
        out.append(keep)
    return jnp.concatenate([o[0] for o in out], axis=0), jnp.concatenate([o[1] for o in out], axis=0)

def factor_block(work, upper, fillers):
    sups = BLK // SUP
    for s in range(sups):
        base = s * SUP
        rows = [slice(base + t * SUB, base + (t + 1) * SUB) for t in range(SUP // SUB)]
        ua, ui = eliminate([work[r, :BLK] for r in rows], [work[r, BLK:] for r in rows], base)
        upper[base : base + SUP, :BLK] = ua
        upper[base : base + SUP, BLK:] = ui
        nxt = base + SUP
        if nxt < BLK:
            done = jnp.concatenate([ua, ui], axis=1)
            hi = done.astype(BF16)
            lo = (done - hi.astype(F32)).astype(BF16)
            left = jnp.concatenate([hi[:, :BLK], hi[:, :BLK], lo[:, :BLK]], axis=0)
            right = jnp.concatenate([hi, lo, hi], axis=0)
            change = lax.dot_general(left, right, (((0,), (0,)), ((), ())), preferred_element_type=F32)
        for filler in fillers[s * len(fillers) // sups : (s + 1) * len(fillers) // sups]:
            filler()
        if nxt < BLK:
            work[nxt:, :] = work[nxt:, :] - change[nxt:, :]


def main_kernel(
    pw, d_in, bins, w1, bias, w2, out, f_hi, f_lo, sq_col, sq_row, sc_col, sc_row, stack, cur, work, upper,
    x_hi, x_lo, inv_hi, inv_lo,
):
    tile = 2 * pw
    row_index, col_index = lax.axis_index("row"), lax.axis_index("col")
    row_start, col_start = row_index * tile, col_index * pw
    feat = w2.shape[1]
    chunks = (2 * tile + pw) // BLK
    lead_chunks = tile // BLK
    starts = [t * BLK for t in range(lead_chunks)]
    starts += [row_start + t * BLK for t in range(lead_chunks)]
    starts += [col_start + t * BLK for t in range(pw // BLK)]
    ones = jnp.ones((SUB, feat), BF16)
    pick = (lax.broadcasted_iota(jnp.int32, (SUB, bins.shape[1] - d_in), 1) == 0).astype(F32).astype(BF16)

    def embed(t):
        start = starts[t]
        at = pl.ds(start if isinstance(start, int) else pl.multiple_of(start, BLK), BLK)
        here = slice(t * BLK, (t + 1) * BLK)
        pre = jnp.dot(bins[at, 0:d_in], w1[...], preferred_element_type=F32) + bias[...]
        hidden = jax.nn.gelu(pre).astype(BF16)
        f = jnp.dot(hidden, w2[...], preferred_element_type=F32)
        f_hi[here, :], f_lo[here, :] = split(f)
        ff = f * f
        sq_col[here, :] = jnp.sum(ff, axis=1, keepdims=True)
        p1 = ff.astype(BF16)
        p2, p3 = split(ff - p1.astype(F32))
        sq_row[:, here] = dot_nt(ones, p1) + (dot_nt(ones, p2) + dot_nt(ones, p3))
        cnt = bins[at, d_in:]
        sc_col[here, :] = jnp.sqrt(cnt[:, 0:1].astype(F32))
        sc_row[:, here] = jnp.sqrt(dot_nt(pick, cnt))

    def window(a0, n, b0, m, left_id, right_id):
        la, rb = pl.ds(a0, n), pl.ds(b0, m)
        inner = dot3((f_hi[la, :], f_lo[la, :]), (f_hi[rb, :], f_lo[rb, :]))
        dist = jnp.maximum(sq_col[la, :] + sq_row[0:1, rb] - 2.0 * inner, 0.0)
        q = dist * (4.0 / feat)
        r = jnp.sqrt(q)
        matern = (1.0 + root_five * r + 5.0 / 3.0 * q) * jnp.exp(-root_five * r)
        ids = left_id + lax.broadcasted_iota(jnp.int32, (n, m), 0)
        jds = right_id + lax.broadcasted_iota(jnp.int32, (n, m), 1)
        return (ids == jds).astype(F32) + sc_col[la, :] * sc_row[0:1, rb] * (matern + kernel_offset)

    def lead_window(t):
        stack[t * BLK : (t + 1) * BLK, :] = window(t * BLK, BLK, 0, tile, starts[t], 0)

    def cur_window(h):
        cur[h * BLK : (h + 1) * BLK, :] = window(
            tile + h * BLK, BLK, 2 * tile, pw, row_start + h * BLK, col_start
        )

    def pair(rows, cols):
        return x_hi[rows, cols], x_lo[rows, cols]

    def place(b):
        return pl.ds(b * BLK if isinstance(b, int) else pl.multiple_of(b * BLK, BLK), BLK)

    def solve(rows, b):
        panel = dot3(split(stack[rows, place(b)]), (inv_hi[...], inv_lo[...]))
        x_hi[rows, place(b)], x_lo[rows, place(b)] = split(panel)

    def reduce(rows, b):
        stack[rows, place(b)] = stack[rows, place(b)] - dot3(
            pair(rows, slice(None)), pair(place(b), slice(None))
        )

    def downdate(h, b):
        rows = slice(tile + h * BLK, tile + (h + 1) * BLK)
        here = slice(h * BLK, (h + 1) * BLK)
        cur[here, :] = cur[here, :] - dot3(pair(rows, place(b)), pair(slice(2 * tile, None), place(b)))

    def finish(b):
        inv_hi[...], inv_lo[...] = split(upper[:, BLK:])
        solve(slice(0, tile), b)

    work[:, BLK:] = (
        lax.broadcasted_iota(jnp.int32, (BLK, BLK), 0) == lax.broadcasted_iota(jnp.int32, (BLK, BLK), 1)
    ).astype(F32)
    for t in range(lead_chunks):
        embed(t)
    for t in range(lead_chunks):
        lead_window(t)
    x_hi[...] = jnp.zeros_like(x_hi)
    x_lo[...] = jnp.zeros_like(x_lo)

    outer = range(lead_chunks, chunks)
    fillers = [lambda t=t: embed(t) for t in outer] + [lambda t=t: lead_window(t) for t in outer]
    fillers += [lambda h=h: cur_window(h) for h in range(lead_chunks)]
    work[:, :BLK] = stack[0:BLK, 0:BLK]
    factor_block(work, upper, fillers)
    finish(0)

    def step(b, carry):
        work[:, :BLK] = stack[place(b), place(b)] - dot3(
            pair(place(b), slice(None)), pair(place(b), slice(None))
        )
        work[:, BLK:] = (
            lax.broadcasted_iota(jnp.int32, (BLK, BLK), 0) == lax.broadcasted_iota(jnp.int32, (BLK, BLK), 1)
        ).astype(F32)

        def advance(t):
            rows = slice(t * BLK, (t + 1) * BLK)
            solve(rows, b - 1)
            reduce(rows, b)

        tasks = [lambda t=t: reduce(slice(t * BLK, (t + 1) * BLK), b) for t in range(lead_chunks)]
        tasks += [lambda t=t: advance(t) for t in outer]
        tasks += [lambda h=h: downdate(h, b - 1) for h in range(lead_chunks)]
        factor_block(work, upper, tasks)
        finish(b)
        return carry

    lax.fori_loop(1, lead_chunks, step, 0)

    is_lead = row_index == 0
    last = lead_chunks - 1

    def write_panel(c):
        cols = slice(c * pw, (c + 1) * pw)

        @pl.when((col_index == c) & is_lead)
        def _():
            ids = lax.broadcasted_iota(jnp.int32, (tile, pw), 0)
            jds = lax.broadcasted_iota(jnp.int32, (tile, pw), 1) + c * pw
            whole = x_hi[0:tile, cols].astype(F32) + x_lo[0:tile, cols].astype(F32)
            out[...] = jnp.where(ids >= jds, whole, 0.0)

        @pl.when((col_index == c) & jnp.logical_not(is_lead))
        def _():
            solve(slice(tile, 2 * tile), last)
            out[...] = x_hi[tile : 2 * tile, cols].astype(F32) + x_lo[tile : 2 * tile, cols].astype(F32)

    write_panel(0)
    write_panel(1)

    @pl.when((col_index >= 2) & is_lead)
    def _():
        out[...] = jnp.zeros((tile, pw), F32)

    @pl.when((col_index >= 2) & jnp.logical_not(is_lead))
    def _():
        solve(slice(tile, None), last)
        out[...] = cur[...] - dot3(
            pair(slice(tile, 2 * tile), place(last)), pair(slice(2 * tile, None), place(last))
        )


def gather_kernel(x_ref, o_ref, own_sem, send_sem, pass_sem, recv_sem):
    rows, cols = lax.axis_size("row"), lax.axis_size("col")
    my_row, my_col = lax.axis_index("row"), lax.axis_index("col")
    me = my_row * cols + my_col
    total = rows * cols
    height = x_ref.shape[0]

    def block(g):
        return o_ref.at[pl.ds(pl.multiple_of(g * height, height), height), :]

    def direct(source, row, col):
        same_row = source // cols == row
        lead = (source // cols == 0) & (source % cols == col)
        return same_row | lead | ((source // cols != 0) & (source // rows == col))

    def needs(source, row, col):
        return direct(source, row, col) | (source // cols == 0)

    def send_copy(target):
        return pltpu.make_async_remote_copy(
            src_ref=x_ref,
            dst_ref=block(me),
            send_sem=send_sem.at[target],
            recv_sem=recv_sem.at[me],
            device_id=(target // cols, target % cols),
            device_id_type=pl.DeviceIdType.MESH,
        )

    barrier = pltpu.get_barrier_semaphore()
    own = pltpu.make_async_copy(x_ref, block(me), own_sem)
    own.start()

    def greet(d, c):
        other = (me + d) % total
        pl.semaphore_signal(
            barrier, inc=1, device_id=(other // cols, other % cols), device_id_type=pl.DeviceIdType.MESH
        )
        return c

    lax.fori_loop(1, total, greet, 0)
    pl.semaphore_wait(barrier, total - 1)

    def send(d, c):
        target = (me + d) % total

        @pl.when(direct(me, target // cols, target % cols))
        def _():
            send_copy(target).start()

        return c

    lax.fori_loop(1, total, send, 0)

    def pass_copy(d):
        to_col = (my_col + d) % cols
        return pltpu.make_async_remote_copy(
            src_ref=block(my_col),
            dst_ref=block(my_col),
            send_sem=pass_sem.at[to_col],
            recv_sem=recv_sem.at[my_col],
            device_id=(my_row, to_col),
            device_id_type=pl.DeviceIdType.MESH,
        )

    @pl.when(my_row != 0)
    def _():
        pltpu.make_async_remote_copy(
            src_ref=x_ref,
            dst_ref=block(my_col),
            send_sem=send_sem.at[my_col],
            recv_sem=recv_sem.at[my_col],
            device_id=(0, my_col),
            device_id_type=pl.DeviceIdType.MESH,
        ).wait_recv()

        def forward(d, c):
            pass_copy(d).start()
            return c

        lax.fori_loop(1, cols, forward, 0)

    own.wait()

    def receive(d, c):
        source = (me + total - d) % total

        @pl.when(needs(source, my_row, my_col) & ((my_row == 0) | (source != my_col)))
        def _():
            pltpu.make_async_remote_copy(
                src_ref=x_ref,
                dst_ref=block(source),
                send_sem=send_sem.at[source],
                recv_sem=recv_sem.at[source],
                device_id=(source // cols, source % cols),
                device_id_type=pl.DeviceIdType.MESH,
            ).wait_recv()

        return c

    lax.fori_loop(1, total, receive, 0)

    def drain(d, c):
        target = (me + d) % total

        @pl.when(direct(me, target // cols, target % cols))
        def _():
            send_copy(target).wait_send()

        return c

    lax.fori_loop(1, total, drain, 0)

    @pl.when(my_row != 0)
    def _():
        def drain_pass(d, c):
            pass_copy(d).wait_send()
            return c

        lax.fori_loop(1, cols, drain_pass, 0)


def gather_bins(packed):
    total = lax.axis_size("row") * lax.axis_size("col")
    anywhere = pl.BlockSpec(memory_space=pl.ANY)
    return pl.pallas_call(
        gather_kernel,
        out_shape=jax.ShapeDtypeStruct((packed.shape[0] * total, packed.shape[1]), packed.dtype),
        in_specs=[anywhere],
        out_specs=anywhere,
        scratch_shapes=[
            pltpu.SemaphoreType.DMA,
            pltpu.SemaphoreType.DMA((total,)),
            pltpu.SemaphoreType.DMA((lax.axis_size("col"),)),
            pltpu.SemaphoreType.DMA((total,)),
        ],
        compiler_params=pltpu.CompilerParams(collective_id=0, has_side_effects=True),
    )(packed)


def per_device(event_bins, counts, hidden_weight, hidden_bias, feature_weight):
    d_in = event_bins.shape[1]
    col_count, row_count = lax.axis_size("col"), lax.axis_size("row")
    tile = event_bins.shape[0] * col_count
    pw = tile * row_count // col_count
    feat = feature_weight.shape[1]
    wide = jnp.broadcast_to(counts.astype(BF16)[:, None], (counts.shape[0], 128 - d_in))
    packed = jnp.concatenate([event_bins, wide], axis=1)
    bins = gather_bins(packed)
    n = 2 * tile + pw
    vm = pl.BlockSpec(memory_space=pltpu.VMEM)
    return pl.pallas_call(
        lambda *refs: main_kernel(pw, d_in, *refs),
        out_shape=jax.ShapeDtypeStruct((tile, pw), F32),
        in_specs=[vm] * 4,
        out_specs=vm,
        scratch_shapes=[
            pltpu.VMEM((n, feat), BF16),
            pltpu.VMEM((n, feat), BF16),
            pltpu.VMEM((n, 1), F32),
            pltpu.VMEM((SUB, n), F32),
            pltpu.VMEM((n, 1), F32),
            pltpu.VMEM((SUB, n), F32),
            pltpu.VMEM((n, tile), F32),
            pltpu.VMEM((tile, pw), F32),
            pltpu.VMEM((BLK, 2 * BLK), F32),
            pltpu.VMEM((BLK, 2 * BLK), F32),
            pltpu.VMEM((n, tile), BF16),
            pltpu.VMEM((n, tile), BF16),
            pltpu.VMEM((BLK, BLK), BF16),
            pltpu.VMEM((BLK, BLK), BF16),
        ],
        compiler_params=pltpu.CompilerParams(vmem_limit_bytes=60 * 1024 * 1024),
    )(bins, hidden_weight, hidden_bias.reshape(1, -1), feature_weight)


def solution(mesh):
    in_specs = (P(("row", "col"), None), P(("row", "col")), P(), P(), P())
    return jax.shard_map(
        per_device, mesh=mesh, in_specs=in_specs, out_specs=P("row", "col"), check_vma=False
    )
```

```python
import math

import jax
import jax.numpy as jnp
from jax import lax
from jax.experimental import pallas as pl
from jax.experimental.pallas import tpu as pltpu
from jax.sharding import PartitionSpec as P

kernel_offset = 0.25
gelu_linear = (2.0 / math.pi) ** 0.5
gelu_cubic = 0.044715 * gelu_linear
log2_e = math.log2(math.e)
tiny = 1e-30
BLK = 128
SUP = 32
SUB = 8
F32 = jnp.float32
BF16 = jnp.bfloat16


def split(x):
    hi = x.astype(BF16)
    return hi, (x - hi.astype(F32)).astype(BF16)


def dot_nt(a, b):
    return lax.dot_general(a, b, (((1,), (1,)), ((), ())), preferred_element_type=F32)


def dot3(a, b):
    return dot_nt(a[0], b[0]) + (dot_nt(a[0], b[1]) + dot_nt(a[1], b[0]))


def spread(x, j):
    return jnp.broadcast_to(x[j : j + 1, :], x.shape)

def eliminate(left, right, base, zero):
    groups = len(left)
    left, right = list(left), list(right)
    sub = lax.broadcasted_iota(jnp.int32, (SUB, BLK), 0)
    out = []
    for k in range(groups):
        col = {}
        for t in range(k, groups):
            for m in range(SUB):
                lane = base + k * SUB + m
                col[t, m] = jnp.broadcast_to(left[t][:, lane : lane + 1], (SUB, BLK))
                if t == k and m < 2:
                    col[t, m] = col[t, m] + zero
        keep = [None, None]
        for j in range(0, SUB, 2):
            a, b = col[k, j], col[k, j + 1]
            p, q, r = spread(a, j), spread(a, j + 1), spread(b, j + 1)
            det = p * r - q * q
            ip, ih = lax.rsqrt(p), lax.rsqrt(det)
            ip_ih = ip * ih
            alpha, beta = r * a - q * b, p * b - q * a
            ih2 = ih * ih
            la, lb = {k: a * ip}, {k: beta * ip_ih}
            for t in range(k + 1, groups):
                la[t] = col[t, j] * ip
                lb[t] = (p * col[t, j + 1] - q * col[t, j]) * ip_ih
            for m in range(j + 2, SUB):
                both = alpha * spread(a, m) + beta * spread(b, m)
                col[k, m] = col[k, m] - both * ih2
                if k + 1 < groups:
                    sa, sb = spread(la[k], m), spread(lb[k], m)
                    for t in range(k + 1, groups):
                        col[t, m] = col[t, m] - (la[t] * sa + lb[t] * sb)
            for h, side in enumerate((left, right)):
                first, second = spread(side[k], j), spread(side[k], j + 1)
                ua = first * ip
                ub = (p * second - q * first) * ip_ih
                keep[h] = ua if j == 0 else jnp.where(sub == j, ua, keep[h])
                keep[h] = jnp.where(sub == j + 1, ub, keep[h])
                for t in range(k if j + 2 < SUB else k + 1, groups):
                    side[t] = side[t] - (la[t] * ua + lb[t] * ub)
        out.append(keep)
    return jnp.concatenate([o[0] for o in out], axis=0), jnp.concatenate([o[1] for o in out], axis=0)

def factor_block(work, upper, zeros, fillers):
    zero = zeros[...]
    sups = BLK // SUP
    for s in range(sups):
        base = s * SUP
        rows = [slice(base + t * SUB, base + (t + 1) * SUB) for t in range(SUP // SUB)]
        ua, ui = eliminate([work[r, :BLK] for r in rows], [work[r, BLK:] for r in rows], base, zero)
        upper[base : base + SUP, :BLK] = ua
        upper[base : base + SUP, BLK:] = ui
        nxt = base + SUP
        if nxt < BLK:
            done = jnp.concatenate([ua, ui], axis=1)
            hi = done.astype(BF16)
            lo = (done - hi.astype(F32)).astype(BF16)
            left = jnp.concatenate([hi[:, :BLK], hi[:, :BLK], lo[:, :BLK]], axis=0)
            right = jnp.concatenate([hi, lo, hi], axis=0)
            change = lax.dot_general(left, right, (((0,), (0,)), ((), ())), preferred_element_type=F32)
        for filler in fillers[s * len(fillers) // sups : (s + 1) * len(fillers) // sups]:
            filler()
        if nxt < BLK:
            work[nxt:, :] = work[nxt:, :] - change[nxt:, :]


def main_kernel(
    pw, d_in, bins, w1, bias, w2, out, feats, sq_col, sq_row, sc_col, sc_row, stack, cur, work, upper,
    x_hi, x_lo, inv_hi, inv_lo, zeros,
):
    tile = 2 * pw
    row_index, col_index = lax.axis_index("row"), lax.axis_index("col")
    row_start, col_start = row_index * tile, col_index * pw
    feat = w2.shape[1]
    reach = (5.0 / feat) ** 0.5
    chunks = (2 * tile + pw) // BLK
    lead_chunks = tile // BLK
    starts = [t * BLK for t in range(lead_chunks)]
    starts += [row_start + t * BLK for t in range(lead_chunks)]
    starts += [col_start + t * BLK for t in range(pw // BLK)]
    ones = jnp.ones((SUB, feat), BF16)
    pick = (lax.broadcasted_iota(jnp.int32, (SUB, bins.shape[1] - d_in), 1) == 0).astype(F32).astype(BF16)

    def embed(t):
        start = starts[t]
        at = pl.ds(start if isinstance(start, int) else pl.multiple_of(start, BLK), BLK)
        here = slice(t * BLK, (t + 1) * BLK)
        pre = jnp.dot(bins[at, 0:d_in], w1[...], preferred_element_type=F32) + bias[...]
        inner = pre * (gelu_linear + gelu_cubic * (pre * pre))
        hidden = (pre * (1.0 + jnp.tanh(inner))).astype(BF16)
        f = (jnp.dot(hidden, w2[...], preferred_element_type=F32) * reach).astype(BF16)
        feats[here, :] = f
        wide = f.astype(F32)
        ff = wide * wide
        sq_col[here, :] = jnp.sum(ff, axis=1, keepdims=True)
        p1, p2 = split(ff)
        sq_row[:, here] = dot_nt(ones, p1) + dot_nt(ones, p2)
        cnt = bins[at, d_in:]
        sc_col[here, :] = jnp.sqrt(cnt[:, 0:1].astype(F32))
        sc_row[:, here] = jnp.sqrt(dot_nt(pick, cnt))

    def window(a0, n, b0, m):
        la, rb = slice(a0, a0 + n), slice(b0, b0 + m)
        inner = dot_nt(feats[la, :] * (-2.0), feats[rb, :])
        t2 = jnp.maximum(sq_col[la, :] + sq_row[0:1, rb] + inner, tiny)
        t = t2 * lax.rsqrt(t2)
        matern = (1.0 + t + t2 * (1.0 / 3.0)) * jnp.exp2(t * (-log2_e))
        return sc_col[la, :] * sc_row[0:1, rb] * (matern + kernel_offset)

    def diagonal(n, m, shift):
        ids = shift + lax.broadcasted_iota(jnp.int32, (n, m), 0)
        return (ids == lax.broadcasted_iota(jnp.int32, (n, m), 1)).astype(F32)

    def lead_window(t):
        part = window(t * BLK, BLK, 0, tile)
        if t < lead_chunks:
            part = part + diagonal(BLK, tile, t * BLK)
        stack[t * BLK : (t + 1) * BLK, :] = part

    def cur_window(h):
        cur[h * BLK : (h + 1) * BLK, :] = window(tile + h * BLK, BLK, 2 * tile, pw) + diagonal(
            BLK, pw, row_start + h * BLK - col_start
        )

    def pair(rows, cols):
        return x_hi[rows, cols], x_lo[rows, cols]

    def place(b):
        return slice(b * BLK, (b + 1) * BLK)

    def solve(rows, b):
        panel = dot3(split(stack[rows, place(b)]), (inv_hi[...], inv_lo[...]))
        x_hi[rows, place(b)], x_lo[rows, place(b)] = split(panel)

    def reduce(rows, b):
        stack[rows, place(b)] = stack[rows, place(b)] - dot3(
            pair(rows, slice(0, b * BLK)), pair(place(b), slice(0, b * BLK))
        )

    def downdate(h, b):
        rows = slice(tile + h * BLK, tile + (h + 1) * BLK)
        here = slice(h * BLK, (h + 1) * BLK)
        cur[here, :] = cur[here, :] - dot3(pair(rows, place(b)), pair(slice(2 * tile, None), place(b)))

    def finish(b):
        inv_hi[...], inv_lo[...] = split(upper[:, BLK:])
        solve(slice(b * BLK, tile), b)

    eye = diagonal(BLK, BLK, 0)
    zeros[...] = jnp.zeros_like(zeros)
    work[:, BLK:] = eye
    for t in range(lead_chunks):
        embed(t)
    for t in range(lead_chunks):
        lead_window(t)

    outer = range(lead_chunks, chunks)
    fillers = [lambda t=t: embed(t) for t in outer] + [lambda t=t: lead_window(t) for t in outer]
    fillers += [lambda h=h: cur_window(h) for h in range(lead_chunks)]
    work[:, :BLK] = stack[0:BLK, 0:BLK]
    factor_block(work, upper, zeros, fillers)
    finish(0)

    def step(b):
        done = slice(0, b * BLK)
        work[:, :BLK] = stack[place(b), place(b)] - dot3(pair(place(b), done), pair(place(b), done))
        work[:, BLK:] = eye

        def advance(t):
            rows = slice(t * BLK, (t + 1) * BLK)
            solve(rows, b - 1)
            reduce(rows, b)

        tasks = [lambda t=t: reduce(slice(t * BLK, (t + 1) * BLK), b) for t in range(b, lead_chunks)]
        tasks += [lambda t=t: advance(t) for t in outer]
        tasks += [lambda h=h: downdate(h, b - 1) for h in range(lead_chunks)]
        factor_block(work, upper, zeros, tasks)
        finish(b)

    for b in range(1, lead_chunks):
        step(b)

    is_lead = row_index == 0
    last = lead_chunks - 1

    def write_panel(c):
        cols = slice(c * pw, (c + 1) * pw)

        @pl.when((col_index == c) & is_lead)
        def _():
            ids = lax.broadcasted_iota(jnp.int32, (tile, pw), 0)
            jds = lax.broadcasted_iota(jnp.int32, (tile, pw), 1) + c * pw
            whole = x_hi[0:tile, cols].astype(F32) + x_lo[0:tile, cols].astype(F32)
            out[...] = jnp.where(ids >= jds, whole, 0.0)

        @pl.when((col_index == c) & jnp.logical_not(is_lead))
        def _():
            solve(slice(tile, 2 * tile), last)
            out[...] = x_hi[tile : 2 * tile, cols].astype(F32) + x_lo[tile : 2 * tile, cols].astype(F32)

    write_panel(0)
    write_panel(1)

    @pl.when((col_index >= 2) & is_lead)
    def _():
        out[...] = jnp.zeros((tile, pw), F32)

    @pl.when((col_index >= 2) & jnp.logical_not(is_lead))
    def _():
        solve(slice(tile, None), last)
        out[...] = cur[...] - dot3(
            pair(slice(tile, 2 * tile), place(last)), pair(slice(2 * tile, None), place(last))
        )


def gather_kernel(x_ref, o_ref, own_sem, send_sem, pass_sem, recv_sem):
    rows, cols = lax.axis_size("row"), lax.axis_size("col")
    my_row, my_col = lax.axis_index("row"), lax.axis_index("col")
    me = my_row * cols + my_col
    total = rows * cols
    height = x_ref.shape[0]

    def block(g):
        return o_ref.at[pl.ds(pl.multiple_of(g * height, height), height), :]

    def direct(source, row, col):
        same_row = source // cols == row
        lead = (source // cols == 0) & (source % cols == col)
        return same_row | lead | ((source // cols != 0) & (source // rows == col))

    def needs(source, row, col):
        return direct(source, row, col) | (source // cols == 0)

    def send_copy(target):
        return pltpu.make_async_remote_copy(
            src_ref=x_ref,
            dst_ref=block(me),
            send_sem=send_sem.at[target],
            recv_sem=recv_sem.at[me],
            device_id=(target // cols, target % cols),
            device_id_type=pl.DeviceIdType.MESH,
        )

    barrier = pltpu.get_barrier_semaphore()
    own = pltpu.make_async_copy(x_ref, block(me), own_sem)
    own.start()

    def greet(d, c):
        other = (me + d) % total
        pl.semaphore_signal(
            barrier, inc=1, device_id=(other // cols, other % cols), device_id_type=pl.DeviceIdType.MESH
        )
        return c

    lax.fori_loop(1, total, greet, 0)
    pl.semaphore_wait(barrier, total - 1)

    def send(d, c):
        target = (me + d) % total

        @pl.when(direct(me, target // cols, target % cols))
        def _():
            send_copy(target).start()

        return c

    lax.fori_loop(1, total, send, 0)

    def pass_copy(d):
        to_col = (my_col + d) % cols
        return pltpu.make_async_remote_copy(
            src_ref=block(my_col),
            dst_ref=block(my_col),
            send_sem=pass_sem.at[to_col],
            recv_sem=recv_sem.at[my_col],
            device_id=(my_row, to_col),
            device_id_type=pl.DeviceIdType.MESH,
        )

    @pl.when(my_row != 0)
    def _():
        pltpu.make_async_remote_copy(
            src_ref=x_ref,
            dst_ref=block(my_col),
            send_sem=send_sem.at[my_col],
            recv_sem=recv_sem.at[my_col],
            device_id=(0, my_col),
            device_id_type=pl.DeviceIdType.MESH,
        ).wait_recv()

        def forward(d, c):
            pass_copy(d).start()
            return c

        lax.fori_loop(1, cols, forward, 0)

    own.wait()

    def receive(d, c):
        source = (me + total - d) % total

        @pl.when(needs(source, my_row, my_col) & ((my_row == 0) | (source != my_col)))
        def _():
            pltpu.make_async_remote_copy(
                src_ref=x_ref,
                dst_ref=block(source),
                send_sem=send_sem.at[source],
                recv_sem=recv_sem.at[source],
                device_id=(source // cols, source % cols),
                device_id_type=pl.DeviceIdType.MESH,
            ).wait_recv()

        return c

    lax.fori_loop(1, total, receive, 0)

    def drain(d, c):
        target = (me + d) % total

        @pl.when(direct(me, target // cols, target % cols))
        def _():
            send_copy(target).wait_send()

        return c

    lax.fori_loop(1, total, drain, 0)

    @pl.when(my_row != 0)
    def _():
        def drain_pass(d, c):
            pass_copy(d).wait_send()
            return c

        lax.fori_loop(1, cols, drain_pass, 0)


def gather_bins(packed):
    total = lax.axis_size("row") * lax.axis_size("col")
    anywhere = pl.BlockSpec(memory_space=pl.ANY)
    return pl.pallas_call(
        gather_kernel,
        out_shape=jax.ShapeDtypeStruct((packed.shape[0] * total, packed.shape[1]), packed.dtype),
        in_specs=[anywhere],
        out_specs=anywhere,
        scratch_shapes=[
            pltpu.SemaphoreType.DMA,
            pltpu.SemaphoreType.DMA((total,)),
            pltpu.SemaphoreType.DMA((lax.axis_size("col"),)),
            pltpu.SemaphoreType.DMA((total,)),
        ],
        compiler_params=pltpu.CompilerParams(collective_id=0, has_side_effects=True),
    )(packed)


def per_device(event_bins, counts, hidden_weight, hidden_bias, feature_weight):
    d_in = event_bins.shape[1]
    col_count, row_count = lax.axis_size("col"), lax.axis_size("row")
    tile = event_bins.shape[0] * col_count
    pw = tile * row_count // col_count
    feat = feature_weight.shape[1]
    wide = jnp.broadcast_to(counts.astype(BF16)[:, None], (counts.shape[0], 128 - d_in))
    packed = jnp.concatenate([event_bins, wide], axis=1)
    bins = gather_bins(packed)
    n = 2 * tile + pw
    vm = pl.BlockSpec(memory_space=pltpu.VMEM)
    return pl.pallas_call(
        lambda *refs: main_kernel(pw, d_in, *refs),
        out_shape=jax.ShapeDtypeStruct((tile, pw), F32),
        in_specs=[vm] * 4,
        out_specs=vm,
        scratch_shapes=[
            pltpu.VMEM((n, feat), BF16),
            pltpu.VMEM((n, 1), F32),
            pltpu.VMEM((SUB, n), F32),
            pltpu.VMEM((n, 1), F32),
            pltpu.VMEM((SUB, n), F32),
            pltpu.VMEM((n, tile), F32),
            pltpu.VMEM((tile, pw), F32),
            pltpu.VMEM((BLK, 2 * BLK), F32),
            pltpu.VMEM((BLK, 2 * BLK), F32),
            pltpu.VMEM((n, tile), BF16),
            pltpu.VMEM((n, tile), BF16),
            pltpu.VMEM((BLK, BLK), BF16),
            pltpu.VMEM((BLK, BLK), BF16),
            pltpu.VMEM((SUB, BLK), F32),
        ],
        compiler_params=pltpu.CompilerParams(vmem_limit_bytes=60 * 1024 * 1024),
    )(bins, hidden_weight, hidden_bias.reshape(1, -1), feature_weight)


def solution(mesh):
    in_specs = (P(("row", "col"), None), P(("row", "col")), P(), P(), P())
    return jax.shard_map(
        per_device, mesh=mesh, in_specs=in_specs, out_specs=P("row", "col"), check_vma=False
    )
```
